128 devices in a mesh: req: 16 (over z, x), ctx: 8 (over y, core).
Axes of the slice: x: 4, y: 4, z: 4, core: 2. Of those that a mesh axis runs over, the one named last changes fastest.
Arguments:
- item_table: bfloat16 [32768, 256], P('req'), may hold values from -6 to 6
- cand_owner: int32 [16, 512, 1], P('req'), may hold values from 0 to 15; in each aligned block of 64 rows (0 to 63, 64 to 127, ..., all dimensions but the last counted through in order) at most 8 rows name the same one
- cand_slot: int32 [16, 512], P('req'), may hold values from 0 to 2047
- w_in: bfloat16 [256, 1024], replicated, may hold values from -0.375 to 0.375
- w_uq: bfloat16 [1024, 2048], replicated, may hold values from -0.1875 to 0.1875
- w_out: bfloat16 [1024, 1024], replicated, may hold values from -0.1875 to 0.1875
- k_cache: bfloat16 [16, 32768, 1024], P('req', 'ctx'), may hold values from -12 to 12
- v_cache: bfloat16 [16, 32768, 1024], P('req', 'ctx'), may hold values from -6 to 6
- hist_len: int32 [16], P('req'), may hold values from 2048 to 32768, as said below
Outputs:
- ranked: bfloat16 [16, 512, 1024], P('req', 'ctx')
The draws below stay inside these ranges and needn't reach their ends.
Inputs may be any that keep to these rules, and one draw needn't show every extreme that they name: `cand_owner`: in each aligned block of 512 / 8 candidates of a user, no owner is named more than 8 times, and in some block one owner is named exactly 8 times. `hist_len`: in every draw some user has the full 32768 events.
All inputs are finite; a program needn't handle non-finite values.
Results may differ from the reference program's by a relative error of at most 0.014.
Values may be sent and summed in bfloat16 or wider, within the bound.
A program may use at most 128 MiB of HBM per device.

```python
import math
import jax
import jax.numpy as jnp
import numpy as np
from jax import lax

DM = 1024
HEADS = 8
DE = 256
CAND = 512
ITEMS_DEV = 2048
DH = 128
USERS = 16
HIST = 32768
ITEMS = 32768
CAP = 8
N_REQ = 16
N_CTX = 8


def draw_hist_len(key, part):
    key_lengths, key_chosen = jax.random.split(key)
    lengths = jax.random.randint(key_lengths, (USERS,), HIST // 16, HIST + 1)
    chosen = jax.random.randint(key_chosen, (), 0, USERS)
    return jnp.where(jnp.arange(USERS) == chosen, HIST, lengths).astype(jnp.int32)


def set_ends(result, stream_key, low, high):
    extent = result.shape
    place = [jax.random.randint(jax.random.fold_in(stream_key, axis), (), 0, extent[axis]) for axis in range(len(extent))]
    result = result.at[tuple(place)].set(low)
    longest = extent.index(max(extent))
    place[longest] = (place[longest] + 1) % extent[longest]
    return result.at[tuple(place)].set(high)


def level_of(stream_key, extent, shards, least, high):
    loudness, own = 1.0, jax.random.fold_in(stream_key, 6)
    for dim, blocks in shards:
        heights = jnp.exp(jax.random.uniform(jax.random.fold_in(own, dim), (blocks,), jnp.float32, least / len(shards), high / len(shards)))
        loudness = loudness * jnp.repeat(heights, extent[dim] // blocks).reshape([-1 if axis == dim else 1 for axis in range(len(extent))])
    return loudness


def routed_block(stream_key, own, number, rows, amount, top, limit, skew):
    sequence = jax.random.permutation(stream_key, amount)
    heavy_load, common = load_shares(amount, rows * top, limit, skew, True), load_shares(amount, rows * top, limit, skew, False)
    places = jnp.arange(amount)

    def named(tallies, rotation):
        used = int((tallies > 0).sum())
        fixed = max(1, used // 4)
        moved = fixed + (places - fixed + rotation * (used - fixed)) % max(1, amount - fixed)
        return jnp.zeros((amount,), jnp.int32).at[sequence[jnp.where(places < fixed, places, moved)]].set(jnp.asarray(tallies, jnp.int32))

    tallies = jnp.where(number % 4 == 0, named(heavy_load, number // 4), named(common, number - number // 4 - 1))
    mixed = jax.random.permutation(jax.random.fold_in(own, 3), amount)
    giver, sink = mixed[0:amount // 2 * 2:2], mixed[1:amount // 2 * 2:2]
    margin = jnp.minimum(tallies[giver] - 1, limit - tallies[sink]) // 2
    margin = jnp.where((giver == sequence[0]) | (sink == sequence[0]) | (tallies[sink] == 0), 0, jnp.maximum(margin, 0))
    moved = jax.random.randint(jax.random.fold_in(own, 4), (amount // 2,), 0, 1 << 20) % (margin + 1)
    tallies = tallies.at[giver].add(-moved).at[sink].add(moved)
    members = jnp.searchsorted(jnp.cumsum(tallies), jnp.arange(rows * top), side="right").astype(jnp.int32)
    table = members.reshape(top, rows).T
    table = table[jax.random.permutation(jax.random.fold_in(own, 1), rows)]
    rotation = jax.random.randint(jax.random.fold_in(own, 2), (rows, 1), 0, top)
    return jnp.take_along_axis(table, (jnp.arange(top)[None, :] + rotation) % top, axis=1)


def load_shares(number_of, total, most, slope, full):
    portions = [(1 << 20) // math.isqrt(grade ** slope) + 1 for grade in range(1, number_of + 1)]
    largest = most if full else min(most, max(-(-total // number_of), total * portions[0] // sum(portions)))
    least = 1 if total - largest >= number_of - 1 else 0
    counts, rest = [largest] + [least] * (number_of - 1), total - largest - least * (number_of - 1)
    while rest > 0:
        free = [i for i in range(1, number_of) if counts[i] < largest] or [i for i in range(1, number_of) if counts[i] < most]
        mass, left = sum([portions[i] for i in free]), rest
        for i in free:
            more = min(most - counts[i], max(1, left * portions[i] // mass), rest)
            counts[i] = counts[i] + more
            rest = rest - more
    return np.array(counts)


def gaussian(key, extent, deviation, reach, pieces=(), held_as=jnp.bfloat16):
    drawn = jax.random.normal(key, extent, jnp.float32) * deviation
    if len(pieces) > 0:
        drawn = level_of(key, extent, pieces, -0.22, 0.18) * drawn
    return jnp.clip(drawn, min=-reach, max=reach).astype(held_as)


def setup_inputs(seed: int = 0) -> dict:
    seeds = jax.random.split(jax.random.key(seed), 10)
    item_table = gaussian(seeds[0], (ITEMS, DE), 1.0, 6.0, ((0, 16),))
    cand_owner_keys = jax.random.split(jax.random.fold_in(seeds[1], 1), USERS * CAND // (CAND // N_CTX))
    cand_owner_turns = jax.random.permutation(jax.random.fold_in(seeds[1], 3), USERS * CAND // (CAND // N_CTX))
    cand_owner = jax.vmap(lambda own, number: routed_block(jax.random.fold_in(seeds[1], 2), own, number, CAND // N_CTX, N_REQ, 1, CAP, 2))(cand_owner_keys, cand_owner_turns).reshape((USERS, CAND, 1))
    cand_slot = set_ends(jax.random.randint(seeds[2], (USERS, CAND), 0, ITEMS_DEV), jax.random.fold_in(seeds[2], 1), 0, ITEMS_DEV - 1).astype(jnp.int32)
    w_in = gaussian(seeds[3], (DE, DM), DE ** -0.5, 0.375)
    w_uq = gaussian(seeds[4], (DM, 2 * DM), DM ** -0.5, 0.1875)
    w_out = gaussian(seeds[5], (DM, DM), DM ** -0.5, 0.1875)
    k_cache = gaussian(seeds[6], (USERS, HIST, DM), 2.0, 12.0, ((0, 16), (1, 8)))
    v_cache = gaussian(seeds[7], (USERS, HIST, DM), 1.0, 6.0, ((0, 16), (1, 8)))
    hist_len = draw_hist_len(jax.random.fold_in(seeds[9], 71), 0)
    return {"item_table": item_table, "cand_owner": cand_owner, "cand_slot": cand_slot, "w_in": w_in, "w_uq": w_uq, "w_out": w_out, "k_cache": k_cache, "v_cache": v_cache, "hist_len": hist_len}


def layer_norm(values):
    centre = lax.optimization_barrier(jnp.mean(values, axis=-1, keepdims=True))
    centred = values - centre
    spread = lax.optimization_barrier(jnp.mean(centred * centred, axis=-1, keepdims=True))
    return centred * lax.rsqrt(spread + 1e-05)

def attend_user(operands):
    query_rows, keys_user, values_user, length = operands
    block_size = math.gcd(HIST, 2048)
    block_count = HIST // block_size
    scale = DH ** (-0.5)
    query_heads = query_rows.reshape(CAND, HEADS, DH).astype(jnp.float32)

    def step(total, index):
        start = (index * block_size).astype(jnp.int32)
        key_block = lax.dynamic_slice_in_dim(keys_user, start, block_size, 0).reshape(block_size, HEADS, DH).astype(jnp.float32)
        value_block = lax.dynamic_slice_in_dim(values_user, start, block_size, 0).reshape(block_size, HEADS, DH).astype(jnp.float32)
        scores = jnp.einsum('qhd,khd->hqk', query_heads, key_block) * scale
        position = start + jnp.arange(block_size).astype(jnp.int32)
        weights = jnp.where(position[None, None, :] < length, jax.nn.silu(scores), 0.0)
        weights = lax.optimization_barrier(weights.astype(jnp.bfloat16)).astype(jnp.float32)
        added = jnp.einsum('hqk,khd->qhd', weights, value_block).reshape(CAND, DM)
        return (total + added, None)
    total, unused = lax.scan(step, jnp.zeros((CAND, DM), jnp.float32), jnp.arange(block_count).astype(jnp.int32))
    return total

def reference(item_table, cand_owner, cand_slot, w_in, w_uq, w_out, k_cache, v_cache, hist_len):
    table_rows = (cand_owner[:, :, 0] * ITEMS_DEV + cand_slot).astype(jnp.int32)
    embedded = item_table[table_rows].reshape(USERS * CAND, DE)
    features = jnp.dot(embedded, w_in, preferred_element_type=jnp.float32).astype(jnp.bfloat16)
    normed = layer_norm(features.astype(jnp.float32)).astype(jnp.bfloat16)
    projected = jax.nn.silu(jnp.dot(normed, w_uq, preferred_element_type=jnp.float32)).astype(jnp.bfloat16)
    gate_u = projected[:, :DM]
    query = projected[:, DM:].reshape(USERS, CAND, DM)
    attended = lax.map(attend_user, (query, k_cache, v_cache, hist_len)).reshape(USERS * CAND, DM)
    mixed = (layer_norm(attended) * gate_u.astype(jnp.float32)).astype(jnp.bfloat16)
    ranked = features.astype(jnp.float32) + jnp.dot(mixed, w_out, preferred_element_type=jnp.float32)
    return ranked.astype(jnp.bfloat16).reshape(USERS, CAND, DM)
```

```python
import jax
import jax.numpy as jnp
from jax import lax
from jax.experimental import pallas as pl
from jax.experimental.pallas import tpu as pltpu
from jax.sharding import PartitionSpec as P

MESH = pl.DeviceIdType.MESH
F32, BF16, I32 = jnp.float32, jnp.bfloat16, jnp.int32
HEADS, DH, WIDTH = 8, 128, 1024
OWNERS, CAP = 16, 8
HALF = 64
PAIR = 2 * HALF
KEYS = 4096
ITEMS = 2048
DE = 256
QSCALE = 0.5 * DH ** (-0.5)


def silu(values):
    half = 0.5 * values
    return half + half * jnp.tanh(half)


def layer_norm(values):
    centre = jnp.mean(values, axis=-1, keepdims=True)
    centred = values - centre
    spread = jnp.mean(centred * centred, axis=-1, keepdims=True)
    return centred * lax.rsqrt(spread + 1e-05)


def ranked_hits(named, wanted):
    shape = (2 * PAIR, PAIR)
    row = lax.broadcasted_iota(I32, shape, 0)
    lane = lax.broadcasted_iota(I32, shape, 1)
    half = lax.rem(lax.div(row, CAP), 2)
    place = lax.rem(row, CAP)
    match = jnp.where((named == wanted) & (lax.div(lane, HALF) == half), 1.0, 0.0)
    upto = jnp.where(
        lax.broadcasted_iota(I32, (PAIR, PAIR), 0) <= lax.broadcasted_iota(I32, (PAIR, PAIR), 1),
        1.0,
        0.0,
    ).astype(BF16)
    rank = jnp.dot(match.astype(BF16), upto, preferred_element_type=F32)
    return jnp.where(rank == (place + 1).astype(F32), match, 0.0)


def kernel(
    owner_ref, slot_ref, len_ref, table_hbm, w_in_hbm, w_uq_hbm, w_out_hbm, k_hbm, v_hbm,
    out_ref,
    owners, slots, table, w_in, w_uq, w_out, keys, vals, rowbuf, got, emb, feat, norm, query,
    acc, own, sbuf, relay, parts,
    load_sem, kv_sem, id_send, id_recv, row_send, row_recv, emb_send, emb_recv,
    part_send, relay_recv, part_recv,
):
    req = lax.axis_index("req")
    ctx = lax.axis_index("ctx")
    y, core = lax.div(ctx, 2), lax.rem(ctx, 2)
    up, down, far = lax.rem(y + 1, 4), lax.rem(y + 3, 4), lax.rem(y + 2, 4)
    partner = y * 2 + 1 - core

    loads = [
        pltpu.make_async_copy(src, dst, load_sem.at[n])
        for n, (src, dst) in enumerate(
            [(table_hbm, table), (w_in_hbm, w_in), (w_uq_hbm, w_uq), (w_out_hbm, w_out)]
        )
    ]

    def kv_copy(which, head):
        src, dst = ((k_hbm, keys), (v_hbm, vals))[which]
        return pltpu.make_async_copy(
            src.at[0, :, pl.ds(pl.multiple_of(head * DH, DH), DH)], dst.at[head], kv_sem.at[which, head]
        )

    barrier = pltpu.get_barrier_semaphore()

    def greet(step, carry):
        pl.semaphore_signal(
            barrier, inc=1, device_id=(lax.rem(req + step, OWNERS), ctx), device_id_type=MESH
        )
        return carry

    lax.fori_loop(1, OWNERS, greet, 0)
    for other in (partner, up * 2, up * 2 + 1, down * 2, down * 2 + 1, far * 2 + core):
        pl.semaphore_signal(barrier, inc=1, device_id=(req, other), device_id_type=MESH)
    for load in loads:
        load.start()
    lanes = pl.ds(pl.multiple_of(y * PAIR, PAIR), PAIR)
    own_ids = [
        pltpu.make_async_copy(owner_ref.at[:, lanes], owners.at[req], id_recv.at[0, req]),
        pltpu.make_async_copy(slot_ref.at[:, lanes], slots.at[req], id_recv.at[1, req]),
    ]
    for copy in own_ids:
        copy.start()
    pl.semaphore_wait(barrier, OWNERS - 1 + 6)

    def id_copy(which, peer, index):
        src, dst = ((owner_ref, owners), (slot_ref, slots))[which]
        return pltpu.make_async_remote_copy(
            src_ref=src.at[:, lanes],
            dst_ref=dst.at[index],
            send_sem=id_send.at[which, peer],
            recv_sem=id_recv.at[which, index],
            device_id=(peer, ctx),
            device_id_type=MESH,
        )

    def send_ids(step, carry):
        peer = lax.rem(req + step, OWNERS)
        id_copy(0, peer, req).start()
        id_copy(1, peer, req).start()
        return carry

    lax.fori_loop(1, OWNERS, send_ids, 0)

    def start_kv(head, carry):
        kv_copy(0, head).start()
        kv_copy(1, head).start()
        return carry

    lax.fori_loop(0, HEADS, start_kv, 0)
    loads[0].wait()
    for copy in own_ids:
        copy.wait()

    def wait_ids(step, carry):
        peer = lax.rem(req + step, OWNERS)
        for which in range(2):
            copy = id_copy(which, peer, peer)
            copy.wait_recv()
        return carry

    lax.fori_loop(1, OWNERS, wait_ids, 0)

    wide = (OWNERS, 2 * CAP, PAIR)
    named = jnp.broadcast_to(owners[...], wide).reshape(2 * PAIR, PAIR)
    asked = jnp.broadcast_to(slots[...], wide).reshape(2 * PAIR, PAIR)
    hits = ranked_hits(named, req)
    chosen = jnp.sum(hits * asked.astype(F32), axis=1, keepdims=True).astype(I32)
    onehot = jnp.where(
        lax.broadcasted_iota(I32, (2 * PAIR, ITEMS), 1) == chosen, 1.0, 0.0
    ).astype(BF16)
    rows = jnp.dot(onehot, table[...], preferred_element_type=F32)
    rowbuf[...] = rows.reshape(OWNERS, 2 * CAP, DE).astype(BF16)

    def row_copy(peer, index):
        return pltpu.make_async_remote_copy(
            src_ref=rowbuf.at[peer],
            dst_ref=got.at[index],
            send_sem=row_send.at[peer],
            recv_sem=row_recv.at[index],
            device_id=(peer, ctx),
            device_id_type=MESH,
        )

    def send_rows(step, carry):
        row_copy(lax.rem(req + step, OWNERS), req).start()
        return carry

    lax.fori_loop(1, OWNERS, send_rows, 0)
    got[req] = rowbuf[req]

    mine = jnp.broadcast_to(owners[req], (2 * PAIR, PAIR))
    giver = lax.div(lax.broadcasted_iota(I32, (2 * PAIR, PAIR), 0), 2 * CAP)
    order = jnp.transpose(ranked_hits(mine, giver)).astype(BF16)

    def wait_kv(head, carry):
        kv_copy(0, head).wait()
        kv_copy(1, head).wait()
        return carry

    lax.fori_loop(0, HEADS, wait_kv, 0)
    live = len_ref[0] - ctx * KEYS
    chunk = 256

    def cut(step, carry):
        start = pl.multiple_of(step * chunk, chunk)
        place = lax.broadcasted_iota(I32, (chunk, DH), 0) + start
        keep = jnp.where(place < live, 1.0, 0.0).astype(BF16)
        for head in range(HEADS):
            vals[head, pl.ds(start, chunk), :] = vals[head, pl.ds(start, chunk), :] * keep
        return carry

    lax.fori_loop(0, KEYS // chunk, cut, 0)
    for load in loads[1:]:
        load.wait()

    def wait_rows(step, carry):
        peer = lax.rem(req + step, OWNERS)
        row_copy(peer, peer).wait_recv()
        return carry

    lax.fori_loop(1, OWNERS, wait_rows, 0)
    emb[0] = jnp.dot(
        order, got[...].reshape(2 * PAIR, DE), preferred_element_type=F32
    ).astype(BF16)

    def emb_copy(block, chip):
        return pltpu.make_async_remote_copy(
            src_ref=emb.at[0],
            dst_ref=emb.at[block],
            send_sem=emb_send.at[block],
            recv_sem=emb_recv.at[block],
            device_id=(req, chip * 2 + core),
            device_id_type=MESH,
        )

    emb_copies = [emb_copy(1, far), emb_copy(2, down), emb_copy(3, up)]
    for copy in emb_copies:
        copy.start()

    def project(block):
        features = jnp.dot(emb[block], w_in[...], preferred_element_type=F32).astype(BF16)
        normed = layer_norm(features.astype(F32)).astype(BF16)
        raw = jnp.dot(normed, w_uq[:, WIDTH:], preferred_element_type=F32)
        scaled = (silu(raw) * QSCALE).astype(BF16)
        for head in range(HEADS):
            query[min(block, 1), head] = scaled[:, head * DH : (head + 1) * DH]
        return features, normed

    def relay_copy(part):
        heads = pl.ds(part * 4, 4)
        return pltpu.make_async_remote_copy(
            src_ref=sbuf.at[1, heads],
            dst_ref=relay.at[heads],
            send_sem=part_send.at[1, part, 0],
            recv_sem=relay_recv.at[part],
            device_id=(req, up * 2 + core),
            device_id_type=MESH,
        )

    def part_copy(block, part, side, chip, slot):
        heads = pl.ds(part * 4, 4)
        rows_there = pl.ds(pl.multiple_of(side * HALF, HALF), HALF)
        return pltpu.make_async_remote_copy(
            src_ref=sbuf.at[block, heads, rows_there],
            dst_ref=parts.at[slot, heads],
            send_sem=part_send.at[block, part, 0 if block == 0 else side],
            recv_sem=part_recv.at[slot, part],
            device_id=(req, chip * 2 + side),
            device_id_type=MESH,
        )

    def step(index, carry):
        block = lax.rem(lax.div(index + 1, 2), 4)
        part = jnp.where(index == 7, 1, jnp.where(index == 0, 0, lax.rem(index + 1, 2)))

        @pl.when(index == 0)
        def _():
            features, normed = project(0)
            feat[...] = features
            norm[...] = normed

        for number, copy in enumerate(emb_copies):

            @pl.when(index == 2 * number + 1)
            def _():
                copy.wait_recv()
                project(number + 1)

        for head in range(4):
            at = part * 4 + head
            score = lax.dot_general(
                query[jnp.minimum(block, 1), at], keys[at], (((1,), (1,)), ((), ())), preferred_element_type=F32
            )
            weight = (score + score * jnp.tanh(score)).astype(BF16)
            acc[head] = jnp.dot(weight, vals[at], preferred_element_type=F32)

        heads = pl.ds(part * 4, 4)

        @pl.when(block == 0)
        def _():
            sbuf[0, heads] = acc[...].astype(BF16)
            own[heads] = acc[:, pl.ds(pl.multiple_of(core * HALF, HALF), HALF), :]
            part_copy(0, part, 1 - core, y, 4).start()

        @pl.when(block == 1)
        def _():
            sbuf[1, heads] = acc[...].astype(BF16)
            relay_copy(part).start()

        @pl.when(block == 2)
        def _():
            relay_copy(part).wait_recv()
            sbuf[2, heads] = (acc[...] + relay[heads].astype(F32)).astype(BF16)
            for side in range(2):
                part_copy(2, part, side, up, core).start()

        @pl.when(block == 3)
        def _():
            sbuf[3, heads] = acc[...].astype(BF16)
            for side in range(2):
                part_copy(3, part, side, down, 2 + core).start()

        return carry

    lax.fori_loop(0, 8, step, 0)

    my_rows = pl.ds(pl.multiple_of(core * HALF, HALF), HALF)
    gate = silu(
        jnp.dot(norm[my_rows, :], w_uq[:, :WIDTH], preferred_element_type=F32)
    ).astype(BF16)
    for part in range(2):
        for slot in range(5):
            part_copy(0, part, 1 - core, y, slot).wait_recv()
    total = own[...]
    for slot in range(5):
        total = total + parts[slot].astype(F32)
    attended = jnp.concatenate([total[head] for head in range(HEADS)], axis=-1)
    mixed = (layer_norm(attended) * gate.astype(F32)).astype(BF16)
    ranked = feat[my_rows, :].astype(F32) + jnp.dot(
        mixed, w_out[...], preferred_element_type=F32
    )
    out_ref[...] = ranked.astype(BF16)

    def drain(step, carry):
        peer = lax.rem(req + step, OWNERS)
        id_copy(0, peer, req).wait_send()
        id_copy(1, peer, req).wait_send()
        row_copy(peer, req).wait_send()
        return carry

    lax.fori_loop(1, OWNERS, drain, 0)
    for copy in emb_copies:
        copy.wait_send()
    for part in range(2):
        part_copy(0, part, 1 - core, y, 4).wait_send()
        relay_copy(part).wait_send()
        for side in range(2):
            part_copy(2, part, side, up, core).wait_send()
            part_copy(3, part, side, down, 2 + core).wait_send()


def shards(item_table, cand_owner, cand_slot, w_in, w_uq, w_out, k_cache, v_cache, hist_len):
    hbm = pl.BlockSpec(memory_space=pl.ANY)
    vmem = pl.BlockSpec(memory_space=pltpu.VMEM)
    smem = pl.BlockSpec(memory_space=pltpu.SMEM)
    dma = pltpu.SemaphoreType.DMA
    out = pl.pallas_call(
        kernel,
        out_shape=jax.ShapeDtypeStruct((HALF, WIDTH), BF16),
        in_specs=[vmem, vmem, smem] + [hbm] * 6,
        out_specs=vmem,
        scratch_shapes=[
            pltpu.VMEM((OWNERS, 1, PAIR), I32),
            pltpu.VMEM((OWNERS, 1, PAIR), I32),
            pltpu.VMEM((ITEMS, DE), BF16),
            pltpu.VMEM((DE, WIDTH), BF16),
            pltpu.VMEM((WIDTH, 2 * WIDTH), BF16),
            pltpu.VMEM((WIDTH, WIDTH), BF16),
            pltpu.VMEM((HEADS, KEYS, DH), BF16),
            pltpu.VMEM((HEADS, KEYS, DH), BF16),
            pltpu.VMEM((OWNERS, 2 * CAP, DE), BF16),
            pltpu.VMEM((OWNERS, 2 * CAP, DE), BF16),
            pltpu.VMEM((4, PAIR, DE), BF16),
            pltpu.VMEM((PAIR, WIDTH), BF16),
            pltpu.VMEM((PAIR, WIDTH), BF16),
            pltpu.VMEM((2, HEADS, PAIR, DH), BF16),
            pltpu.VMEM((4, PAIR, DH), F32),
            pltpu.VMEM((HEADS, HALF, DH), F32),
            pltpu.VMEM((4, HEADS, PAIR, DH), BF16),
            pltpu.VMEM((HEADS, PAIR, DH), BF16),
            pltpu.VMEM((5, HEADS, HALF, DH), BF16),
            dma((4,)),
            dma((2, HEADS)),
            dma((2, OWNERS)),
            dma((2, OWNERS)),
            dma((OWNERS,)),
            dma((OWNERS,)),
            dma((4,)),
            dma((4,)),
            dma((4, 2, 2)),
            dma((2,)),
            dma((5, 2)),
        ],
        compiler_params=pltpu.CompilerParams(
            collective_id=0, has_side_effects=True, vmem_limit_bytes=56 * 2**20
        ),
    )(
        cand_owner.reshape(1, cand_owner.shape[1]),
        cand_slot,
        hist_len,
        item_table,
        w_in,
        w_uq,
        w_out,
        k_cache,
        v_cache,
    )
    return out[None]


def solution(mesh):
    in_specs = (
        P("req", None),
        P("req", None, None),
        P("req", None),
        P(),
        P(),
        P(),
        P("req", "ctx", None),
        P("req", "ctx", None),
        P("req"),
    )
    out_specs = P("req", "ctx", None)
    return jax.shard_map(shards, mesh=mesh, in_specs=in_specs, out_specs=out_specs, check_vma=False)
```

```python
import jax
import jax.numpy as jnp
from jax import lax
from jax.experimental import pallas as pl
from jax.experimental.pallas import tpu as pltpu
from jax.sharding import PartitionSpec as P

MESH = pl.DeviceIdType.MESH
F32, BF16, I32 = jnp.float32, jnp.bfloat16, jnp.int32
HEADS, DH, WIDTH = 8, 128, 1024
OWNERS, CAP = 16, 8
HALF = 64
PAIR = 2 * HALF
KEYS = 4096
ITEMS = 2048
DE = 256
QSCALE = 0.5 * DH ** (-0.5)


def silu(values):
    half = 0.5 * values
    return half + half * jnp.tanh(half)


def layer_norm(values):
    centre = jnp.mean(values, axis=-1, keepdims=True)
    centred = values - centre
    spread = jnp.mean(centred * centred, axis=-1, keepdims=True)
    return centred * lax.rsqrt(spread + 1e-05)


def ranked_hits(named, wanted):
    shape = (2 * PAIR, PAIR)
    row = lax.broadcasted_iota(I32, shape, 0)
    lane = lax.broadcasted_iota(I32, shape, 1)
    half = lax.rem(lax.div(row, CAP), 2)
    place = lax.rem(row, CAP)
    match = jnp.where((named == wanted) & (lax.div(lane, HALF) == half), 1.0, 0.0)
    upto = jnp.where(
        lax.broadcasted_iota(I32, (PAIR, PAIR), 0) <= lax.broadcasted_iota(I32, (PAIR, PAIR), 1),
        1.0,
        0.0,
    ).astype(BF16)
    rank = jnp.dot(match.astype(BF16), upto, preferred_element_type=F32)
    return jnp.where(rank == (place + 1).astype(F32), match, 0.0)


def kernel(
    owner_hbm, slot_hbm, len_ref, table_hbm, w_in_hbm, w_uq_hbm, w_out_hbm, k_hbm, v_hbm,
    out_ref,
    owners, slots, table, w_in, w_uq, w_out, keys, vals, rowbuf, got, emb, feat, norm, query,
    query_wide, acc, mine, theirs, swapped, sums, parts,
    load_sem, kv_sem, id_send, id_recv, row_send, row_recv, emb_send, emb_recv,
    swap_send, swap_recv, part_send, part_recv,
):
    req = lax.axis_index("req")
    ctx = lax.axis_index("ctx")
    y, core = lax.div(ctx, 2), lax.rem(ctx, 2)
    up, down, far = lax.rem(y + 1, 4), lax.rem(y + 3, 4), lax.rem(y + 2, 4)
    partner = y * 2 + 1 - core

    loads = [
        pltpu.make_async_copy(src, dst, load_sem.at[n])
        for n, (src, dst) in enumerate(
            [(table_hbm, table), (w_in_hbm, w_in), (w_uq_hbm, w_uq), (w_out_hbm, w_out)]
        )
    ]

    def kv_copy(which, head):
        src, dst = ((k_hbm, keys), (v_hbm, vals))[which]
        return pltpu.make_async_copy(
            src.at[0, :, pl.ds(pl.multiple_of(head * DH, DH), DH)], dst.at[head], kv_sem.at[which, head]
        )

    barrier = pltpu.get_barrier_semaphore()

    def greet(step, carry):
        pl.semaphore_signal(
            barrier, inc=1, device_id=(lax.rem(req + step, OWNERS), ctx), device_id_type=MESH
        )
        return carry

    lax.fori_loop(1, OWNERS, greet, 0)
    for other in (partner, up * 2 + core, down * 2 + core, far * 2 + core):
        pl.semaphore_signal(barrier, inc=1, device_id=(req, other), device_id_type=MESH)
    lanes = pl.ds(pl.multiple_of(y * PAIR, PAIR), PAIR)
    own_ids = [
        pltpu.make_async_copy(owner_hbm.at[:, lanes], owners.at[req], id_recv.at[0, req]),
        pltpu.make_async_copy(slot_hbm.at[:, lanes], slots.at[req], id_recv.at[1, req]),
    ]
    for copy in [*own_ids, *loads]:
        copy.start()
    for copy in own_ids:
        copy.wait()
    pl.semaphore_wait(barrier, OWNERS - 1 + 4)

    def id_copy(which, peer, index):
        ids = (owners, slots)[which]
        return pltpu.make_async_remote_copy(
            src_ref=ids.at[req],
            dst_ref=ids.at[index],
            send_sem=id_send.at[which, peer],
            recv_sem=id_recv.at[which, index],
            device_id=(peer, ctx),
            device_id_type=MESH,
        )

    def send_ids(step, carry):
        peer = lax.rem(req + step, OWNERS)
        id_copy(0, peer, req).start()
        id_copy(1, peer, req).start()
        return carry

    lax.fori_loop(1, OWNERS, send_ids, 0)

    def start_kv(head, carry):
        kv_copy(0, head).start()
        kv_copy(1, head).start()
        return carry

    lax.fori_loop(0, HEADS, start_kv, 0)
    loads[0].wait()

    def wait_ids(step, carry):
        peer = lax.rem(req + step, OWNERS)
        for which in range(2):
            copy = id_copy(which, peer, peer)
            copy.wait_recv()
        return carry

    lax.fori_loop(1, OWNERS, wait_ids, 0)

    wide = (OWNERS, 2 * CAP, PAIR)
    named = jnp.broadcast_to(owners[...], wide).reshape(2 * PAIR, PAIR)
    asked = jnp.broadcast_to(slots[...], wide).reshape(2 * PAIR, PAIR)
    hits = ranked_hits(named, req)
    chosen = jnp.sum(hits * asked.astype(F32), axis=1, keepdims=True).astype(I32)
    onehot = jnp.where(
        lax.broadcasted_iota(I32, (2 * PAIR, ITEMS), 1) == chosen, 1.0, 0.0
    ).astype(BF16)
    rows = jnp.dot(onehot, table[...], preferred_element_type=F32)
    rowbuf[...] = rows.reshape(OWNERS, 2 * CAP, DE).astype(BF16)

    def row_copy(peer, index):
        return pltpu.make_async_remote_copy(
            src_ref=rowbuf.at[peer],
            dst_ref=got.at[index],
            send_sem=row_send.at[peer],
            recv_sem=row_recv.at[index],
            device_id=(peer, ctx),
            device_id_type=MESH,
        )

    def send_rows(step, carry):
        row_copy(lax.rem(req + step, OWNERS), req).start()
        return carry

    lax.fori_loop(1, OWNERS, send_rows, 0)
    got[req] = rowbuf[req]

    asked_here = jnp.broadcast_to(owners[req], (2 * PAIR, PAIR))
    giver = lax.div(lax.broadcasted_iota(I32, (2 * PAIR, PAIR), 0), 2 * CAP)
    order = jnp.transpose(ranked_hits(asked_here, giver)).astype(BF16)

    def wait_kv(head, carry):
        kv_copy(0, head).wait()
        kv_copy(1, head).wait()
        return carry

    lax.fori_loop(0, HEADS, wait_kv, 0)
    live = len_ref[0] - ctx * KEYS
    chunk = 256

    def cut(step, carry):
        start = pl.multiple_of(step * chunk, chunk)
        place = lax.broadcasted_iota(I32, (chunk, DH), 0) + start
        keep = jnp.where(place < live, 1.0, 0.0).astype(BF16)
        for head in range(HEADS):
            vals[head, pl.ds(start, chunk), :] = vals[head, pl.ds(start, chunk), :] * keep
        return carry

    lax.fori_loop(0, KEYS // chunk, cut, 0)
    for load in loads[1:]:
        load.wait()

    def wait_rows(step, carry):
        peer = lax.rem(req + step, OWNERS)
        row_copy(peer, peer).wait_recv()
        return carry

    lax.fori_loop(1, OWNERS, wait_rows, 0)
    emb[0] = jnp.dot(
        order, got[...].reshape(2 * PAIR, DE), preferred_element_type=F32
    ).astype(BF16)

    def emb_copy(block, chip):
        return pltpu.make_async_remote_copy(
            src_ref=emb.at[0],
            dst_ref=emb.at[block],
            send_sem=emb_send.at[block],
            recv_sem=emb_recv.at[block],
            device_id=(req, chip * 2 + core),
            device_id_type=MESH,
        )

    emb_copies = [emb_copy(1, far), emb_copy(2, down), emb_copy(3, up)]
    for copy in emb_copies:
        copy.start()

    def project(rows_in):
        features = jnp.dot(rows_in, w_in[...], preferred_element_type=F32).astype(BF16)
        normed = layer_norm(features.astype(F32)).astype(BF16)
        raw = jnp.dot(normed, w_uq[:, WIDTH:], preferred_element_type=F32)
        return features, normed, (silu(raw) * QSCALE).astype(BF16)

    def keep_query(buffer, scaled):
        for head in range(HEADS):
            buffer[head] = scaled[:, head * DH : (head + 1) * DH]

    my_rows = pl.ds(pl.multiple_of(core * HALF, HALF), HALF)
    their_rows = pl.ds(pl.multiple_of((1 - core) * HALF, HALF), HALF)

    def swap_copy(block, pair):
        heads = pl.ds(pair * 2, 2)
        return pltpu.make_async_remote_copy(
            src_ref=theirs.at[block, heads],
            dst_ref=swapped.at[block, heads],
            send_sem=swap_send.at[block, pair],
            recv_sem=swap_recv.at[block, pair],
            device_id=(req, partner),
            device_id_type=MESH,
        )

    def hand_over(block, pair, first):
        heads = pl.ds(pair * 2, 2)
        mine[block, heads] = acc[first : first + 2, my_rows, :]
        theirs[block, heads] = acc[first : first + 2, their_rows, :].astype(BF16)
        swap_copy(block, pair).start()

    def sum_copy(block, pair):
        heads = pl.ds(pair * 2, 2)
        return pltpu.make_async_remote_copy(
            src_ref=sums.at[block, heads],
            dst_ref=parts.at[block, heads],
            send_sem=part_send.at[block, pair],
            recv_sem=part_recv.at[block, pair],
            device_id=(req, (y, far, up, down)[block] * 2 + core),
            device_id_type=MESH,
        )

    def finish(block, pair):
        heads = pl.ds(pair * 2, 2)
        swap_copy(block, pair).wait_recv()
        sums[block, heads] = (mine[block, heads] + swapped[block, heads].astype(F32)).astype(BF16)
        sum_copy(block, pair).start()

    def attend(asking, head):
        score = lax.dot_general(
            asking, keys[head], (((1,), (1,)), ((), ())), preferred_element_type=F32
        )
        weight = (score + score * jnp.tanh(score)).astype(BF16)
        return jnp.dot(weight, vals[head], preferred_element_type=F32)

    features, normed, scaled = project(emb[0])
    feat[...] = features
    norm[...] = normed
    keep_query(query.at[0], scaled)
    for head in range(4):
        acc[head] = attend(query[0, head], head)
    for pair in range(2):
        hand_over(0, pair, 2 * pair)

    for copy in emb_copies[:2]:
        copy.wait_recv()
    keep_query(query_wide, project(emb[1:3].reshape(2 * PAIR, DE))[2])
    piece = 512
    pieces = KEYS // piece

    def wide_step(pair, carry):
        def scored(item):
            head = pair * 2 + item // pieces
            start = (item % pieces) * piece
            return lax.dot_general(
                keys[head, start : start + piece, :],
                query_wide[head],
                (((1,), (1,)), ((), ())),
                preferred_element_type=F32,
            )

        score = scored(0)
        total = None
        for item in range(2 * pieces):
            ahead = scored(item + 1) if item + 1 < 2 * pieces else None
            weight = (score + score * jnp.tanh(score)).astype(BF16)
            start = (item % pieces) * piece
            added = lax.dot_general(
                vals[pair * 2 + item // pieces, start : start + piece, :],
                weight,
                (((0,), (0,)), ((), ())),
                preferred_element_type=F32,
            )
            total = added if item % pieces == 0 else total + added
            if item % pieces == pieces - 1:
                turned = jnp.transpose(total)
                acc[item // pieces] = turned[:PAIR]
                acc[2 + item // pieces] = turned[PAIR:]
            score = ahead
        hand_over(1, pair, 0)
        hand_over(2, pair, 2)

        @pl.when(pair > 0)
        def _():
            finish(1, pair - 1)
            finish(2, pair - 1)

        return carry

    lax.fori_loop(0, 4, wide_step, 0)

    emb_copies[2].wait_recv()
    keep_query(query.at[1], project(emb[3])[2])

    def last_step(index, carry):
        other = index < 4
        block = jnp.where(other, 3, 0)
        pair = jnp.where(other, index, index - 2)
        which = jnp.where(other, 1, 0)
        for head in range(2):
            acc[head] = attend(query[which, pair * 2 + head], pair * 2 + head)
        hand_over(block, pair, 0)

        @pl.when(index == 0)
        def _():
            finish(1, 3)
            finish(2, 3)

        @pl.when((index > 0) & (index < 5))
        def _():
            finish(3, index - 1)

        return carry

    lax.fori_loop(0, 6, last_step, 0)

    gate = silu(
        jnp.dot(norm[my_rows, :], w_uq[:, :WIDTH], preferred_element_type=F32)
    ).astype(BF16)
    for pair in range(4):
        swap_copy(0, pair).wait_recv()
        for block in range(1, 4):
            sum_copy(block, pair).wait_recv()
    total = mine[0] + swapped[0].astype(F32)
    for block in range(1, 4):
        total = total + parts[block].astype(F32)
    attended = jnp.concatenate([total[head] for head in range(HEADS)], axis=-1)
    mixed = (layer_norm(attended) * gate.astype(F32)).astype(BF16)
    ranked = feat[my_rows, :].astype(F32) + jnp.dot(
        mixed, w_out[...], preferred_element_type=F32
    )
    out_ref[...] = ranked.astype(BF16)

    def drain(step, carry):
        peer = lax.rem(req + step, OWNERS)
        id_copy(0, peer, req).wait_send()
        id_copy(1, peer, req).wait_send()
        row_copy(peer, req).wait_send()
        return carry

    lax.fori_loop(1, OWNERS, drain, 0)
    for copy in emb_copies:
        copy.wait_send()
    for pair in range(4):
        for block in range(4):
            swap_copy(block, pair).wait_send()
        for block in range(1, 4):
            sum_copy(block, pair).wait_send()


def shards(item_table, cand_owner, cand_slot, w_in, w_uq, w_out, k_cache, v_cache, hist_len):
    hbm = pl.BlockSpec(memory_space=pl.ANY)
    vmem = pl.BlockSpec(memory_space=pltpu.VMEM)
    dma = pltpu.SemaphoreType.DMA
    out = pl.pallas_call(
        kernel,
        out_shape=pltpu.VMEM((HALF, WIDTH), BF16),
        in_specs=[hbm, hbm, pl.BlockSpec(memory_space=pltpu.SMEM)] + [hbm] * 6,
        out_specs=vmem,
        scratch_shapes=[
            pltpu.VMEM((OWNERS, 1, PAIR), I32),
            pltpu.VMEM((OWNERS, 1, PAIR), I32),
            pltpu.VMEM((ITEMS, DE), BF16),
            pltpu.VMEM((DE, WIDTH), BF16),
            pltpu.VMEM((WIDTH, 2 * WIDTH), BF16),
            pltpu.VMEM((WIDTH, WIDTH), BF16),
            pltpu.VMEM((HEADS, KEYS, DH), BF16),
            pltpu.VMEM((HEADS, KEYS, DH), BF16),
            pltpu.VMEM((OWNERS, 2 * CAP, DE), BF16),
            pltpu.VMEM((OWNERS, 2 * CAP, DE), BF16),
            pltpu.VMEM((4, PAIR, DE), BF16),
            pltpu.VMEM((PAIR, WIDTH), BF16),
            pltpu.VMEM((PAIR, WIDTH), BF16),
            pltpu.VMEM((2, HEADS, PAIR, DH), BF16),
            pltpu.VMEM((HEADS, 2 * PAIR, DH), BF16),
            pltpu.VMEM((4, PAIR, DH), F32),
            pltpu.VMEM((4, HEADS, HALF, DH), F32),
            pltpu.VMEM((4, HEADS, HALF, DH), BF16),
            pltpu.VMEM((4, HEADS, HALF, DH), BF16),
            pltpu.VMEM((4, HEADS, HALF, DH), BF16),
            pltpu.VMEM((4, HEADS, HALF, DH), BF16),
            dma((4,)),
            dma((2, HEADS)),
            dma((2, OWNERS)),
            dma((2, OWNERS)),
            dma((OWNERS,)),
            dma((OWNERS,)),
            dma((4,)),
            dma((4,)),
            dma((4, 4)),
            dma((4, 4)),
            dma((4, 4)),
            dma((4, 4)),
        ],
        compiler_params=pltpu.CompilerParams(
            collective_id=0, has_side_effects=True, vmem_limit_bytes=56 * 2**20
        ),
    )(
        cand_owner.reshape(1, cand_owner.shape[1]),
        cand_slot,
        hist_len,
        item_table,
        w_in,
        w_uq,
        w_out,
        k_cache,
        v_cache,
    )
    return out[None]


def solution(mesh):
    in_specs = (
        P("req", None),
        P("req", None, None),
        P("req", None),
        P(),
        P(),
        P(),
        P("req", "ctx", None),
        P("req", "ctx", None),
        P("req"),
    )
    out_specs = P("req", "ctx", None)
    return jax.shard_map(shards, mesh=mesh, in_specs=in_specs, out_specs=out_specs, check_vma=False)
```

```python
import jax
import jax.numpy as jnp
from jax import lax
from jax.experimental import pallas as pl
from jax.experimental.pallas import tpu as pltpu
from jax.sharding import PartitionSpec as P

MESH = pl.DeviceIdType.MESH
F32, BF16, I32 = jnp.float32, jnp.bfloat16, jnp.int32
HEADS, DH, WIDTH = 8, 128, 1024
OWNERS, CAP = 16, 8
HALF = 64
PAIR = 2 * HALF
KEYS = 4096
ITEMS = 2048
DE = 256
QSCALE = 0.5 * DH ** (-0.5)


def silu(values):
    half = 0.5 * values
    return half + half * jnp.tanh(half)


def layer_norm(values):
    centre = jnp.mean(values, axis=-1, keepdims=True)
    centred = values - centre
    spread = jnp.mean(centred * centred, axis=-1, keepdims=True)
    return centred * lax.rsqrt(spread + 1e-05)


def ranked_hits(named, wanted):
    shape = (2 * PAIR, PAIR)
    row = lax.broadcasted_iota(I32, shape, 0)
    lane = lax.broadcasted_iota(I32, shape, 1)
    half = lax.rem(lax.div(row, CAP), 2)
    place = lax.rem(row, CAP)
    match = jnp.where((named == wanted) & (lax.div(lane, HALF) == half), 1.0, 0.0)
    upto = jnp.where(
        lax.broadcasted_iota(I32, (PAIR, PAIR), 0) <= lax.broadcasted_iota(I32, (PAIR, PAIR), 1),
        1.0,
        0.0,
    ).astype(BF16)
    rank = jnp.dot(match.astype(BF16), upto, preferred_element_type=F32)
    return jnp.where(rank == (place + 1).astype(F32), match, 0.0)


def kernel(
    owner_hbm, slot_hbm, len_ref, table_hbm, w_in_hbm, w_uq_hbm, w_out_hbm, k_hbm, v_hbm,
    out_ref,
    ids, table, w_in, w_uq, w_out, keys, vals, rowbuf, got, emb, feat, norm, query,
    query_wide, acc, mine, theirs, swapped, sums, parts,
    load_sem, kv_sem, id_load, id_send, id_recv, row_send, row_recv, emb_send, emb_recv,
    swap_send, swap_recv, part_send, part_recv,
):
    req = lax.axis_index("req")
    ctx = lax.axis_index("ctx")
    y, core = lax.div(ctx, 2), lax.rem(ctx, 2)
    up, down, far = lax.rem(y + 1, 4), lax.rem(y + 3, 4), lax.rem(y + 2, 4)
    partner = y * 2 + 1 - core

    loads = [
        pltpu.make_async_copy(src, dst, load_sem.at[n])
        for n, (src, dst) in enumerate(
            [(table_hbm, table), (w_in_hbm, w_in), (w_uq_hbm, w_uq), (w_out_hbm, w_out)]
        )
    ]

    def kv_copy(which, head):
        src, dst = ((k_hbm, keys), (v_hbm, vals))[which]
        return pltpu.make_async_copy(
            src.at[0, :, pl.ds(pl.multiple_of(head * DH, DH), DH)], dst.at[head], kv_sem.at[which, head]
        )

    barrier = pltpu.get_barrier_semaphore()

    z, x = lax.div(req, 4), lax.rem(req, 4)
    offsets = sorted(
        [(dz, dx) for dz in range(4) for dx in range(4) if dz or dx],
        key=lambda way: -min(way[0], 4 - way[0]) - min(way[1], 4 - way[1]),
    )
    peers = [lax.rem(z + dz, 4) * 4 + lax.rem(x + dx, 4) for dz, dx in offsets]
    for peer in peers:
        pl.semaphore_signal(barrier, inc=1, device_id=(peer, ctx), device_id_type=MESH)
    for other in (partner, up * 2 + core, down * 2 + core, far * 2 + core):
        pl.semaphore_signal(barrier, inc=1, device_id=(req, other), device_id_type=MESH)
    asked_chip = jnp.where(core == 0, y, far)
    lanes = pl.ds(pl.multiple_of(asked_chip * PAIR, PAIR), PAIR)
    own_ids = [
        pltpu.make_async_copy(src.at[:, lanes], ids.at[req, which], id_load.at[which])
        for which, src in enumerate((owner_hbm, slot_hbm))
    ]
    for copy in [*own_ids, *loads]:
        copy.start()
    for copy in own_ids:
        copy.wait()
    pl.semaphore_wait(barrier, OWNERS - 1 + 4)

    def id_copy(peer, index):
        return pltpu.make_async_remote_copy(
            src_ref=ids.at[req],
            dst_ref=ids.at[index],
            send_sem=id_send.at[peer],
            recv_sem=id_recv.at[index],
            device_id=(peer, ctx),
            device_id_type=MESH,
        )

    for peer in peers:
        id_copy(peer, req).start()

    def start_kv(head, carry):
        kv_copy(0, head).start()
        kv_copy(1, head).start()
        return carry

    lax.fori_loop(0, HEADS, start_kv, 0)
    loads[0].wait()

    def wait_ids(step, carry):
        peer = lax.rem(req + step, OWNERS)
        id_copy(peer, peer).wait_recv()
        return carry

    lax.fori_loop(1, OWNERS, wait_ids, 0)

    wide = (OWNERS, 2 * CAP, PAIR)
    named = jnp.broadcast_to(ids[:, 0], wide).reshape(2 * PAIR, PAIR)
    asked = jnp.broadcast_to(ids[:, 1], wide).reshape(2 * PAIR, PAIR)
    hits = ranked_hits(named, req)
    chosen = jnp.sum(hits * asked.astype(F32), axis=1, keepdims=True).astype(I32)
    onehot = jnp.where(
        lax.broadcasted_iota(I32, (2 * PAIR, ITEMS), 1) == chosen, 1.0, 0.0
    ).astype(BF16)
    rows = jnp.dot(onehot, table[...], preferred_element_type=F32)
    rowbuf[...] = rows.reshape(OWNERS, 2 * CAP, DE).astype(BF16)

    def row_copy(peer, index):
        return pltpu.make_async_remote_copy(
            src_ref=rowbuf.at[peer],
            dst_ref=got.at[index],
            send_sem=row_send.at[peer],
            recv_sem=row_recv.at[index],
            device_id=(peer, ctx),
            device_id_type=MESH,
        )

    for peer in peers:
        row_copy(peer, req).start()
    got[req] = rowbuf[req]

    asked_here = jnp.broadcast_to(ids[req, 0], (2 * PAIR, PAIR))
    giver = lax.div(lax.broadcasted_iota(I32, (2 * PAIR, PAIR), 0), 2 * CAP)
    order = jnp.transpose(ranked_hits(asked_here, giver)).astype(BF16)

    def wait_kv(head, carry):
        kv_copy(0, head).wait()
        kv_copy(1, head).wait()
        return carry

    lax.fori_loop(0, HEADS, wait_kv, 0)
    live = len_ref[0] - ctx * KEYS
    chunk = 256

    def cut(step, carry):
        start = pl.multiple_of(step * chunk, chunk)
        place = lax.broadcasted_iota(I32, (chunk, DH), 0) + start
        keep = jnp.where(place < live, 1.0, 0.0).astype(BF16)
        for head in range(HEADS):
            vals[head, pl.ds(start, chunk), :] = vals[head, pl.ds(start, chunk), :] * keep
        return carry

    lax.fori_loop(0, KEYS // chunk, cut, 0)
    for load in loads[1:]:
        load.wait()

    def wait_rows(step, carry):
        peer = lax.rem(req + step, OWNERS)
        row_copy(peer, peer).wait_recv()
        return carry

    lax.fori_loop(1, OWNERS, wait_rows, 0)
    emb[core] = jnp.dot(
        order, got[...].reshape(2 * PAIR, DE), preferred_element_type=F32
    ).astype(BF16)

    def emb_copy(source, block, there):
        return pltpu.make_async_remote_copy(
            src_ref=emb.at[source],
            dst_ref=emb.at[block],
            send_sem=emb_send.at[block],
            recv_sem=emb_recv.at[block],
            device_id=(req, there),
            device_id_type=MESH,
        )

    emb_given = emb_copy(core, core, partner)
    emb_given.start()
    def project(rows_in):
        features = jnp.dot(rows_in, w_in[...], preferred_element_type=F32).astype(BF16)
        normed = layer_norm(features.astype(F32)).astype(BF16)
        raw = jnp.dot(normed, w_uq[:, WIDTH:], preferred_element_type=F32)
        return features, normed, (silu(raw) * QSCALE).astype(BF16)

    def keep_query(buffer, scaled):
        for head in range(HEADS):
            buffer[head] = scaled[:, head * DH : (head + 1) * DH]

    my_rows = pl.ds(pl.multiple_of(core * HALF, HALF), HALF)
    their_rows = pl.ds(pl.multiple_of((1 - core) * HALF, HALF), HALF)

    def swap_copy(block, pair):
        heads = pl.ds(pair * 2, 2)
        return pltpu.make_async_remote_copy(
            src_ref=theirs.at[block, heads],
            dst_ref=swapped.at[block, heads],
            send_sem=swap_send.at[block, pair],
            recv_sem=swap_recv.at[block, pair],
            device_id=(req, partner),
            device_id_type=MESH,
        )

    def hand_over(block, pair, first):
        heads = pl.ds(pair * 2, 2)
        mine[block, heads] = acc[first : first + 2, my_rows, :]
        theirs[block, heads] = acc[first : first + 2, their_rows, :].astype(BF16)
        swap_copy(block, pair).start()

    def sum_copy(block, pair):
        heads = pl.ds(pair * 2, 2)
        return pltpu.make_async_remote_copy(
            src_ref=sums.at[block, heads],
            dst_ref=parts.at[block, heads],
            send_sem=part_send.at[block, pair],
            recv_sem=part_recv.at[block, pair],
            device_id=(req, (y, far, up, down)[block] * 2 + core),
            device_id_type=MESH,
        )

    def finish(block, pair):
        heads = pl.ds(pair * 2, 2)
        swap_copy(block, pair).wait_recv()
        sums[block, heads] = (mine[block, heads] + swapped[block, heads].astype(F32)).astype(BF16)
        sum_copy(block, pair).start()

    def weigh(score):
        return (score + score * jnp.tanh(score)).astype(BF16)

    piece = 512
    pieces = KEYS // piece

    def attend_two(pair):
        def scored(item):
            start = (item % pieces) * piece
            return lax.dot_general(
                keys[pair * 2 + item // pieces, start : start + piece, :],
                query_wide[pair * 2 + item // pieces],
                (((1,), (1,)), ((), ())),
                preferred_element_type=F32,
            )

        score = scored(0)
        total = None
        for item in range(2 * pieces):
            ahead = scored(item + 1) if item + 1 < 2 * pieces else None
            start = (item % pieces) * piece
            added = lax.dot_general(
                vals[pair * 2 + item // pieces, start : start + piece, :],
                weigh(score),
                (((0,), (0,)), ((), ())),
                preferred_element_type=F32,
            )
            total = added if item % pieces == 0 else total + added
            if item % pieces == pieces - 1:
                turned = jnp.transpose(total)
                acc[item // pieces] = turned[:PAIR]
                acc[2 + item // pieces] = turned[PAIR:]
            score = ahead
        hand_over(2, pair, 0)
        hand_over(3, pair, 2)

    def attend_one(block, pair):
        for head in range(2):
            score = lax.dot_general(
                query[block, pair * 2 + head],
                keys[pair * 2 + head],
                (((1,), (1,)), ((), ())),
                preferred_element_type=F32,
            )
            acc[head] = jnp.dot(
                weigh(score), vals[pair * 2 + head], preferred_element_type=F32
            )
        hand_over(block, pair, 0)

    def open_block(block):
        features, normed, scaled = project(emb[block])
        feat[block] = features
        norm[block] = normed
        keep_query(query.at[block], scaled)
        attend_one(block, 0)

    open_block(core)
    emb_copy(1 - core, 1 - core, partner).wait_recv()
    emb_copies = [emb_copy(0, 2, down * 2 + core), emb_copy(0, 3, up * 2 + core)]
    for copy in emb_copies:
        copy.start()
    open_block(1 - core)

    def far_step(pair, carry):
        attend_one(1, pair)
        finish(1, pair - 1)
        return carry

    lax.fori_loop(1, 4, far_step, 0)

    for copy in emb_copies:
        copy.wait_recv()
    keep_query(query_wide, project(emb[2:4].reshape(2 * PAIR, DE))[2])

    def side_step(pair, carry):
        attend_two(pair)

        @pl.when(pair == 0)
        def _():
            finish(1, 3)

        @pl.when(pair > 0)
        def _():
            finish(2, pair - 1)
            finish(3, pair - 1)

        return carry

    lax.fori_loop(0, 4, side_step, 0)

    def own_step(pair, carry):
        attend_one(0, pair)

        @pl.when(pair == 1)
        def _():
            finish(2, 3)
            finish(3, 3)

        return carry

    lax.fori_loop(1, 4, own_step, 0)

    gate = silu(
        jnp.dot(norm[0, my_rows, :], w_uq[:, :WIDTH], preferred_element_type=F32)
    ).astype(BF16)
    for pair in range(4):
        swap_copy(0, pair).wait_recv()
        for block in range(1, 4):
            sum_copy(block, pair).wait_recv()
    total = mine[0] + swapped[0].astype(F32)
    for block in range(1, 4):
        total = total + parts[block].astype(F32)
    attended = jnp.concatenate([total[head] for head in range(HEADS)], axis=-1)
    mixed = (layer_norm(attended) * gate.astype(F32)).astype(BF16)
    ranked = feat[0, my_rows, :].astype(F32) + jnp.dot(
        mixed, w_out[...], preferred_element_type=F32
    )
    out_ref[...] = ranked.astype(BF16)

    def drain(step, carry):
        peer = lax.rem(req + step, OWNERS)
        id_copy(peer, req).wait_send()
        row_copy(peer, req).wait_send()
        return carry

    lax.fori_loop(1, OWNERS, drain, 0)
    for copy in [emb_given, *emb_copies]:
        copy.wait_send()
    for pair in range(4):
        for block in range(4):
            swap_copy(block, pair).wait_send()
        for block in range(1, 4):
            sum_copy(block, pair).wait_send()


def shards(item_table, cand_owner, cand_slot, w_in, w_uq, w_out, k_cache, v_cache, hist_len):
    hbm = pl.BlockSpec(memory_space=pl.ANY)
    vmem = pl.BlockSpec(memory_space=pltpu.VMEM)
    dma = pltpu.SemaphoreType.DMA
    out = pl.pallas_call(
        kernel,
        out_shape=pltpu.VMEM((HALF, WIDTH), BF16),
        in_specs=[hbm, hbm, pl.BlockSpec(memory_space=pltpu.SMEM)] + [hbm] * 6,
        out_specs=vmem,
        scratch_shapes=[
            pltpu.VMEM((OWNERS, 2, 1, PAIR), I32),
            pltpu.VMEM((ITEMS, DE), BF16),
            pltpu.VMEM((DE, WIDTH), BF16),
            pltpu.VMEM((WIDTH, 2 * WIDTH), BF16),
            pltpu.VMEM((WIDTH, WIDTH), BF16),
            pltpu.VMEM((HEADS, KEYS, DH), BF16),
            pltpu.VMEM((HEADS, KEYS, DH), BF16),
            pltpu.VMEM((OWNERS, 2 * CAP, DE), BF16),
            pltpu.VMEM((OWNERS, 2 * CAP, DE), BF16),
            pltpu.VMEM((4, PAIR, DE), BF16),
            pltpu.VMEM((2, PAIR, WIDTH), BF16),
            pltpu.VMEM((2, PAIR, WIDTH), BF16),
            pltpu.VMEM((2, HEADS, PAIR, DH), BF16),
            pltpu.VMEM((HEADS, 2 * PAIR, DH), BF16),
            pltpu.VMEM((4, PAIR, DH), F32),
            pltpu.VMEM((4, HEADS, HALF, DH), F32),
            pltpu.VMEM((4, HEADS, HALF, DH), BF16),
            pltpu.VMEM((4, HEADS, HALF, DH), BF16),
            pltpu.VMEM((4, HEADS, HALF, DH), BF16),
            pltpu.VMEM((4, HEADS, HALF, DH), BF16),
            dma((4,)),
            dma((2, HEADS)),
            dma((2,)),
            dma((OWNERS,)),
            dma((OWNERS,)),
            dma((OWNERS,)),
            dma((OWNERS,)),
            dma((4,)),
            dma((4,)),
            dma((4, 4)),
            dma((4, 4)),
            dma((4, 4)),
            dma((4, 4)),
        ],
        compiler_params=pltpu.CompilerParams(
            collective_id=0, has_side_effects=True, vmem_limit_bytes=56 * 2**20
        ),
    )(
        cand_owner.reshape(1, cand_owner.shape[1]),
        cand_slot,
        hist_len,
        item_table,
        w_in,
        w_uq,
        w_out,
        k_cache,
        v_cache,
    )
    return out[None]


def solution(mesh):
    in_specs = (
        P("req", None),
        P("req", None, None),
        P("req", None),
        P(),
        P(),
        P(),
        P("req", "ctx", None),
        P("req", "ctx", None),
        P("req"),
    )
    out_specs = P("req", "ctx", None)
    return jax.shard_map(shards, mesh=mesh, in_specs=in_specs, out_specs=out_specs, check_vma=False)
```

```python
import jax
import jax.numpy as jnp
from jax import lax
from jax.experimental import pallas as pl
from jax.experimental.pallas import tpu as pltpu
from jax.sharding import PartitionSpec as P

MESH = pl.DeviceIdType.MESH
F32, BF16, I32 = jnp.float32, jnp.bfloat16, jnp.int32
HEADS, DH, WIDTH = 8, 128, 1024
OWNERS, CAP = 16, 8
HALF = 64
PAIR = 2 * HALF
KEYS = 4096
ITEMS = 2048
DE = 256
QSCALE = 0.5 * DH ** (-0.5)


def silu(values):
    half = 0.5 * values
    return half + half * jnp.tanh(half)


def layer_norm(values):
    centre = jnp.mean(values, axis=-1, keepdims=True)
    centred = values - centre
    spread = jnp.mean(centred * centred, axis=-1, keepdims=True)
    return centred * lax.rsqrt(spread + 1e-05)


def ranked_hits(named, wanted):
    shape = named.shape
    row = lax.broadcasted_iota(I32, shape, 0)
    lane = lax.broadcasted_iota(I32, shape, 1)
    half = lax.rem(lax.div(row, CAP), 2)
    place = lax.rem(row, CAP)
    match = jnp.where((named == wanted) & (lax.div(lane, HALF) == half), 1.0, 0.0)
    upto = jnp.where(
        lax.broadcasted_iota(I32, (PAIR, PAIR), 0) <= lax.broadcasted_iota(I32, (PAIR, PAIR), 1),
        1.0,
        0.0,
    ).astype(BF16)
    rank = jnp.dot(match.astype(BF16), upto, preferred_element_type=F32)
    return jnp.where(rank == (place + 1).astype(F32), match, 0.0)


def kernel(
    owner_hbm, slot_hbm, len_ref, table_hbm, w_in_hbm, w_uq_hbm, w_out_hbm, k_hbm, v_hbm,
    out_ref,
    ids, table, w_in, w_uq, w_out, keys, vals, rowbuf, got, emb, feat, norm, query,
    query_wide, acc, mine, theirs, swapped, sums, parts,
    load_sem, kv_sem, id_load, id_send, id_recv, row_send, row_recv, emb_send, emb_recv,
    swap_send, swap_recv, part_send, part_recv,
):
    req = lax.axis_index("req")
    ctx = lax.axis_index("ctx")
    y, core = lax.div(ctx, 2), lax.rem(ctx, 2)
    up, down, far = lax.rem(y + 1, 4), lax.rem(y + 3, 4), lax.rem(y + 2, 4)
    partner = y * 2 + 1 - core

    loads = [
        pltpu.make_async_copy(src, dst, load_sem.at[n])
        for n, (src, dst) in enumerate(
            [(table_hbm, table), (w_in_hbm, w_in), (w_uq_hbm, w_uq), (w_out_hbm, w_out)]
        )
    ]

    def kv_copy(which, head):
        src, dst = ((k_hbm, keys), (v_hbm, vals))[which]
        return pltpu.make_async_copy(
            src.at[0, :, pl.ds(pl.multiple_of(head * DH, DH), DH)], dst.at[head], kv_sem.at[which, head]
        )

    barrier = pltpu.get_barrier_semaphore()

    z, x = lax.div(req, 4), lax.rem(req, 4)
    offsets = sorted(
        [(dz, dx) for dz in range(4) for dx in range(4)],
        key=lambda way: min(way[0], 4 - way[0]) + min(way[1], 4 - way[1]),
    )
    peers = [lax.rem(z + dz, 4) * 4 + lax.rem(x + dx, 4) for dz, dx in offsets]
    seen_from = [offsets.index((-dz % 4, -dx % 4)) for dz, dx in offsets]
    others = range(OWNERS - 1, 0, -1)
    for place in others:
        pl.semaphore_signal(barrier, inc=1, device_id=(peers[place], ctx), device_id_type=MESH)
    for other in (partner, up * 2 + core, down * 2 + core, far * 2 + core):
        pl.semaphore_signal(barrier, inc=1, device_id=(req, other), device_id_type=MESH)
    asked_chip = jnp.where(core == 0, y, far)
    lanes = pl.ds(pl.multiple_of(asked_chip * PAIR, PAIR), PAIR)
    own_ids = [
        pltpu.make_async_copy(src.at[:, lanes], ids.at[0, which], id_load.at[which])
        for which, src in enumerate((owner_hbm, slot_hbm))
    ]
    for copy in [*own_ids, *loads]:
        copy.start()
    for copy in own_ids:
        copy.wait()
    pl.semaphore_wait(barrier, OWNERS - 1 + 4)

    def id_copy(place, there):
        return pltpu.make_async_remote_copy(
            src_ref=ids.at[0],
            dst_ref=ids.at[there],
            send_sem=id_send.at[place],
            recv_sem=id_recv.at[there],
            device_id=(peers[place], ctx),
            device_id_type=MESH,
        )

    for place in others:
        id_copy(place, seen_from[place]).start()

    def start_kv(head, carry):
        kv_copy(0, head).start()
        kv_copy(1, head).start()
        return carry

    lax.fori_loop(0, HEADS, start_kv, 0)
    loads[0].wait()

    def row_copy(place):
        return pltpu.make_async_remote_copy(
            src_ref=rowbuf.at[place],
            dst_ref=got.at[req],
            send_sem=row_send.at[place],
            recv_sem=row_recv.at[req],
            device_id=(peers[place], ctx),
            device_id_type=MESH,
        )

    def look_up(first, count):
        wide = (count, 2 * CAP, PAIR)
        flat = (count * 2 * CAP, PAIR)
        named = jnp.broadcast_to(ids[first : first + count, 0], wide).reshape(flat)
        asked = jnp.broadcast_to(ids[first : first + count, 1], wide).reshape(flat)
        hits = ranked_hits(named, req)
        chosen = jnp.sum(hits * asked.astype(F32), axis=1, keepdims=True).astype(I32)
        onehot = jnp.where(
            lax.broadcasted_iota(I32, (flat[0], ITEMS), 1) == chosen, 1.0, 0.0
        ).astype(BF16)
        rows = jnp.dot(onehot, table[...], preferred_element_type=F32)
        rowbuf[first : first + count] = rows.reshape(count, 2 * CAP, DE).astype(BF16)

    near = 8
    for place in range(1, near):
        id_copy(place, place).wait_recv()
    look_up(0, near)
    for place in range(near - 1, 0, -1):
        row_copy(place).start()
    for place in range(near, OWNERS):
        id_copy(place, place).wait_recv()
    look_up(near, OWNERS - near)
    for place in range(OWNERS - 1, near - 1, -1):
        row_copy(place).start()
    got[req] = rowbuf[0]

    asked_here = jnp.broadcast_to(ids[0, 0], (2 * PAIR, PAIR))
    giver = lax.div(lax.broadcasted_iota(I32, (2 * PAIR, PAIR), 0), 2 * CAP)
    order = jnp.transpose(ranked_hits(asked_here, giver)).astype(BF16)

    def wait_kv(head, carry):
        kv_copy(0, head).wait()
        kv_copy(1, head).wait()
        return carry

    lax.fori_loop(0, HEADS, wait_kv, 0)
    live = len_ref[0] - ctx * KEYS
    chunk = 256

    def cut(step, carry):
        start = pl.multiple_of(step * chunk, chunk)
        place = lax.broadcasted_iota(I32, (chunk, DH), 0) + start
        keep = jnp.where(place < live, 1.0, 0.0).astype(BF16)
        for head in range(HEADS):
            vals[head, pl.ds(start, chunk), :] = vals[head, pl.ds(start, chunk), :] * keep
        return carry

    lax.fori_loop(0, KEYS // chunk, cut, 0)
    for load in loads[1:]:
        load.wait()

    def came(peer):
        return pltpu.make_async_remote_copy(
            src_ref=rowbuf.at[0],
            dst_ref=got.at[peer],
            send_sem=row_send.at[0],
            recv_sem=row_recv.at[peer],
            device_id=(peer, ctx),
            device_id_type=MESH,
        )

    for place in others:
        came(peers[place]).wait_recv()
    emb[core] = jnp.dot(
        order, got[...].reshape(2 * PAIR, DE), preferred_element_type=F32
    ).astype(BF16)

    def emb_copy(source, block, there):
        return pltpu.make_async_remote_copy(
            src_ref=emb.at[source],
            dst_ref=emb.at[block],
            send_sem=emb_send.at[block],
            recv_sem=emb_recv.at[block],
            device_id=(req, there),
            device_id_type=MESH,
        )

    emb_given = emb_copy(core, core, partner)
    emb_given.start()
    def project(rows_in):
        features = jnp.dot(rows_in, w_in[...], preferred_element_type=F32).astype(BF16)
        normed = layer_norm(features.astype(F32)).astype(BF16)
        raw = jnp.dot(normed, w_uq[:, WIDTH:], preferred_element_type=F32)
        return features, normed, (silu(raw) * QSCALE).astype(BF16)

    def keep_query(buffer, scaled):
        for head in range(HEADS):
            buffer[head] = scaled[:, head * DH : (head + 1) * DH]

    my_rows = pl.ds(pl.multiple_of(core * HALF, HALF), HALF)
    their_rows = pl.ds(pl.multiple_of((1 - core) * HALF, HALF), HALF)

    def swap_copy(block, pair):
        heads = pl.ds(pair * 2, 2)
        return pltpu.make_async_remote_copy(
            src_ref=theirs.at[block, heads],
            dst_ref=swapped.at[block, heads],
            send_sem=swap_send.at[block, pair],
            recv_sem=swap_recv.at[block, pair],
            device_id=(req, partner),
            device_id_type=MESH,
        )

    def hand_over(block, pair, first):
        heads = pl.ds(pair * 2, 2)
        mine[block, heads] = acc[first : first + 2, my_rows, :]
        theirs[block, heads] = acc[first : first + 2, their_rows, :].astype(BF16)
        swap_copy(block, pair).start()

    def sum_copy(block, pair):
        heads = pl.ds(pair * 2, 2)
        return pltpu.make_async_remote_copy(
            src_ref=sums.at[block, heads],
            dst_ref=parts.at[block, heads],
            send_sem=part_send.at[block, pair],
            recv_sem=part_recv.at[block, pair],
            device_id=(req, (y, far, up, down)[block] * 2 + core),
            device_id_type=MESH,
        )

    def finish(block, pair):
        heads = pl.ds(pair * 2, 2)
        swap_copy(block, pair).wait_recv()
        sums[block, heads] = (mine[block, heads] + swapped[block, heads].astype(F32)).astype(BF16)
        sum_copy(block, pair).start()

    def weigh(score):
        return (score + score * jnp.tanh(score)).astype(BF16)

    piece = 512
    pieces = KEYS // piece

    def attend_two(quad):
        def scored(item):
            start = (item % pieces) * piece
            return lax.dot_general(
                keys[quad * 4 + item // pieces, start : start + piece, :],
                query_wide[quad * 4 + item // pieces],
                (((1,), (1,)), ((), ())),
                preferred_element_type=F32,
            )

        score = scored(0)
        total = None
        for item in range(4 * pieces):
            ahead = scored(item + 1) if item + 1 < 4 * pieces else None
            start = (item % pieces) * piece
            added = lax.dot_general(
                vals[quad * 4 + item // pieces, start : start + piece, :],
                weigh(score),
                (((0,), (0,)), ((), ())),
                preferred_element_type=F32,
            )
            total = added if item % pieces == 0 else total + added
            if item % pieces == pieces - 1:
                turned = jnp.transpose(total)
                acc[item // pieces] = turned[:PAIR]
                acc[4 + item // pieces] = turned[PAIR:]
            score = ahead
        for side in range(2):
            for part in range(2):
                hand_over(2 + side, quad * 2 + part, 4 * side + 2 * part)

    def attend_one(block, pair, count=1):
        for head in range(2 * count):
            score = lax.dot_general(
                query[block, pair * 2 + head],
                keys[pair * 2 + head],
                (((1,), (1,)), ((), ())),
                preferred_element_type=F32,
            )
            acc[head] = jnp.dot(
                weigh(score), vals[pair * 2 + head], preferred_element_type=F32
            )
        for part in range(count):
            hand_over(block, pair + part, 2 * part)

    def open_block(block):
        features, normed, scaled = project(emb[block])
        feat[block] = features
        norm[block] = normed
        keep_query(query.at[block], scaled)
        attend_one(block, 0)

    open_block(core)
    emb_copy(1 - core, 1 - core, partner).wait_recv()
    emb_copies = [emb_copy(0, 2, down * 2 + core), emb_copy(0, 3, up * 2 + core)]
    for copy in emb_copies:
        copy.start()
    open_block(1 - core)

    attend_one(1, 1, 3)
    finish(1, 0)

    for copy in emb_copies:
        copy.wait_recv()
    keep_query(query_wide, project(emb[2:4].reshape(2 * PAIR, DE))[2])

    def side_step(quad, carry):
        attend_two(quad)

        @pl.when(quad == 0)
        def _():
            for pair in range(1, 4):
                finish(1, pair)

        @pl.when(quad == 1)
        def _():
            for pair in range(2):
                finish(2, pair)
                finish(3, pair)

        return carry

    lax.fori_loop(0, 2, side_step, 0)

    def own_step(pair, carry):
        attend_one(0, pair)

        @pl.when(pair == 1)
        def _():
            for late in range(2, 4):
                finish(2, late)
                finish(3, late)

        return carry

    lax.fori_loop(1, 4, own_step, 0)

    gate = silu(
        jnp.dot(norm[0, my_rows, :], w_uq[:, :WIDTH], preferred_element_type=F32)
    ).astype(BF16)
    for pair in range(4):
        swap_copy(0, pair).wait_recv()
        for block in range(1, 4):
            sum_copy(block, pair).wait_recv()
    total = mine[0] + swapped[0].astype(F32)
    for block in range(1, 4):
        total = total + parts[block].astype(F32)
    attended = jnp.concatenate([total[head] for head in range(HEADS)], axis=-1)
    mixed = (layer_norm(attended) * gate.astype(F32)).astype(BF16)
    ranked = feat[0, my_rows, :].astype(F32) + jnp.dot(
        mixed, w_out[...], preferred_element_type=F32
    )
    out_ref[...] = ranked.astype(BF16)

    for place in others:
        id_copy(place, seen_from[place]).wait_send()
        row_copy(place).wait_send()
    for copy in [emb_given, *emb_copies]:
        copy.wait_send()
    for pair in range(4):
        for block in range(4):
            swap_copy(block, pair).wait_send()
        for block in range(1, 4):
            sum_copy(block, pair).wait_send()


def shards(item_table, cand_owner, cand_slot, w_in, w_uq, w_out, k_cache, v_cache, hist_len):
    hbm = pl.BlockSpec(memory_space=pl.ANY)
    vmem = pl.BlockSpec(memory_space=pltpu.VMEM)
    dma = pltpu.SemaphoreType.DMA
    out = pl.pallas_call(
        kernel,
        out_shape=pltpu.VMEM((HALF, WIDTH), BF16),
        in_specs=[hbm, hbm, pl.BlockSpec(memory_space=pltpu.SMEM)] + [hbm] * 6,
        out_specs=vmem,
        scratch_shapes=[
            pltpu.VMEM((OWNERS, 2, 1, PAIR), I32),
            pltpu.VMEM((ITEMS, DE), BF16),
            pltpu.VMEM((DE, WIDTH), BF16),
            pltpu.VMEM((WIDTH, 2 * WIDTH), BF16),
            pltpu.VMEM((WIDTH, WIDTH), BF16),
            pltpu.VMEM((HEADS, KEYS, DH), BF16),
            pltpu.VMEM((HEADS, KEYS, DH), BF16),
            pltpu.VMEM((OWNERS, 2 * CAP, DE), BF16),
            pltpu.VMEM((OWNERS, 2 * CAP, DE), BF16),
            pltpu.VMEM((4, PAIR, DE), BF16),
            pltpu.VMEM((2, PAIR, WIDTH), BF16),
            pltpu.VMEM((2, PAIR, WIDTH), BF16),
            pltpu.VMEM((2, HEADS, PAIR, DH), BF16),
            pltpu.VMEM((HEADS, 2 * PAIR, DH), BF16),
            pltpu.VMEM((8, PAIR, DH), F32),
            pltpu.VMEM((4, HEADS, HALF, DH), F32),
            pltpu.VMEM((4, HEADS, HALF, DH), BF16),
            pltpu.VMEM((4, HEADS, HALF, DH), BF16),
            pltpu.VMEM((4, HEADS, HALF, DH), BF16),
            pltpu.VMEM((4, HEADS, HALF, DH), BF16),
            dma((4,)),
            dma((2, HEADS)),
            dma((2,)),
            dma((OWNERS,)),
            dma((OWNERS,)),
            dma((OWNERS,)),
            dma((OWNERS,)),
            dma((4,)),
            dma((4,)),
            dma((4, 4)),
            dma((4, 4)),
            dma((4, 4)),
            dma((4, 4)),
        ],
        compiler_params=pltpu.CompilerParams(
            collective_id=0, has_side_effects=True, vmem_limit_bytes=56 * 2**20
        ),
    )(
        cand_owner.reshape(1, cand_owner.shape[1]),
        cand_slot,
        hist_len,
        item_table,
        w_in,
        w_uq,
        w_out,
        k_cache,
        v_cache,
    )
    return out[None]


def solution(mesh):
    in_specs = (
        P("req", None),
        P("req", None, None),
        P("req", None),
        P(),
        P(),
        P(),
        P("req", "ctx", None),
        P("req", "ctx", None),
        P("req"),
    )
    out_specs = P("req", "ctx", None)
    return jax.shard_map(shards, mesh=mesh, in_specs=in_specs, out_specs=out_specs, check_vma=False)
```

```python
import jax
import jax.numpy as jnp
from jax import lax
from jax.experimental import pallas as pl
from jax.experimental.pallas import tpu as pltpu
from jax.sharding import PartitionSpec as P

MESH = pl.DeviceIdType.MESH
F32, BF16, I32 = jnp.float32, jnp.bfloat16, jnp.int32
HEADS, DH, WIDTH = 8, 128, 1024
OWNERS, CAP = 16, 8
HALF = 64
PAIR = 2 * HALF
KEYS = 4096
ITEMS = 2048
DE = 256
QSCALE = 0.5 * DH ** (-0.5)


def silu(values):
    half = 0.5 * values
    return half + half * jnp.tanh(half)


def layer_norm(values):
    centre = jnp.mean(values, axis=-1, keepdims=True)
    centred = values - centre
    spread = jnp.mean(centred * centred, axis=-1, keepdims=True)
    return centred * lax.rsqrt(spread + 1e-05)


def ranked_hits(named, wanted):
    shape = named.shape
    row = lax.broadcasted_iota(I32, shape, 0)
    lane = lax.broadcasted_iota(I32, shape, 1)
    half = lax.rem(lax.div(row, CAP), 2)
    place = lax.rem(row, CAP)
    match = jnp.where((named == wanted) & (lax.div(lane, HALF) == half), 1.0, 0.0)
    upto = jnp.where(
        lax.broadcasted_iota(I32, (PAIR, PAIR), 0) <= lax.broadcasted_iota(I32, (PAIR, PAIR), 1),
        1.0,
        0.0,
    ).astype(BF16)
    rank = jnp.dot(match.astype(BF16), upto, preferred_element_type=F32)
    return jnp.where(rank == (place + 1).astype(F32), match, 0.0)


def kernel(
    owner_hbm, slot_hbm, len_ref, table_hbm, w_in_hbm, w_uq_hbm, w_out_hbm, k_hbm, v_hbm,
    out_ref,
    ids, table, w_in, w_uq, w_out, keys, vals, rowbuf, got, emb, feat, norm, query,
    query_wide, acc, mine, theirs, swapped, sums, parts,
    load_sem, kv_sem, id_load, id_send, id_recv, row_send, row_recv, emb_send, emb_recv,
    swap_send, swap_recv, part_send, part_recv,
):
    req = lax.axis_index("req")
    ctx = lax.axis_index("ctx")
    y, core = lax.div(ctx, 2), lax.rem(ctx, 2)
    up, down, far = lax.rem(y + 1, 4), lax.rem(y + 3, 4), lax.rem(y + 2, 4)
    partner = y * 2 + 1 - core

    loads = [
        pltpu.make_async_copy(src, dst, load_sem.at[n])
        for n, (src, dst) in enumerate(
            [(table_hbm, table), (w_in_hbm, w_in), (w_uq_hbm, w_uq), (w_out_hbm, w_out)]
        )
    ]

    def kv_copy(which, head):
        src, dst = ((k_hbm, keys), (v_hbm, vals))[which]
        return pltpu.make_async_copy(
            src.at[0, :, pl.ds(pl.multiple_of(head * DH, DH), DH)], dst.at[head], kv_sem.at[which, head]
        )

    barrier = pltpu.get_barrier_semaphore()

    z, x = lax.div(req, 4), lax.rem(req, 4)
    offsets = sorted(
        [(dz, dx) for dz in range(4) for dx in range(4)],
        key=lambda way: min(way[0], 4 - way[0]) + min(way[1], 4 - way[1]),
    )
    peers = [lax.rem(z + dz, 4) * 4 + lax.rem(x + dx, 4) for dz, dx in offsets]
    seen_from = [offsets.index((-dz % 4, -dx % 4)) for dz, dx in offsets]
    others = range(OWNERS - 1, 0, -1)
    for place in others:
        pl.semaphore_signal(barrier, inc=1, device_id=(peers[place], ctx), device_id_type=MESH)
    for other in (partner, up * 2 + core, down * 2 + core, far * 2 + core):
        pl.semaphore_signal(barrier, inc=1, device_id=(req, other), device_id_type=MESH)
    asked_chip = jnp.where(core == 0, y, far)
    lanes = pl.ds(pl.multiple_of(asked_chip * PAIR, PAIR), PAIR)
    own_ids = [
        pltpu.make_async_copy(src.at[:, lanes], ids.at[0, which], id_load.at[which])
        for which, src in enumerate((owner_hbm, slot_hbm))
    ]
    for copy in [*own_ids, *loads]:
        copy.start()
    for copy in own_ids:
        copy.wait()
    pl.semaphore_wait(barrier, OWNERS - 1 + 4)

    def id_copy(place, there):
        return pltpu.make_async_remote_copy(
            src_ref=ids.at[0],
            dst_ref=ids.at[there],
            send_sem=id_send.at[place],
            recv_sem=id_recv.at[there],
            device_id=(peers[place], ctx),
            device_id_type=MESH,
        )

    for place in others:
        id_copy(place, seen_from[place]).start()

    def start_kv(head, carry):
        kv_copy(0, head).start()
        kv_copy(1, head).start()
        return carry

    lax.fori_loop(0, HEADS, start_kv, 0)
    loads[0].wait()

    def row_copy(place):
        return pltpu.make_async_remote_copy(
            src_ref=rowbuf.at[place],
            dst_ref=got.at[req],
            send_sem=row_send.at[place],
            recv_sem=row_recv.at[req],
            device_id=(peers[place], ctx),
            device_id_type=MESH,
        )

    def look_up(first, count):
        wide = (count, 2 * CAP, PAIR)
        flat = (count * 2 * CAP, PAIR)
        named = jnp.broadcast_to(ids[first : first + count, 0], wide).reshape(flat)
        asked = jnp.broadcast_to(ids[first : first + count, 1], wide).reshape(flat)
        hits = ranked_hits(named, req)
        chosen = jnp.sum(hits * asked.astype(F32), axis=1, keepdims=True).astype(I32)
        onehot = jnp.where(
            lax.broadcasted_iota(I32, (flat[0], ITEMS), 1) == chosen, 1.0, 0.0
        ).astype(BF16)
        rows = jnp.dot(onehot, table[...], preferred_element_type=F32)
        rowbuf[first : first + count] = rows.reshape(count, 2 * CAP, DE).astype(BF16)

    near = 11
    for place in range(1, near):
        id_copy(place, place).wait_recv()
    look_up(0, near)
    for place in range(near - 1, 0, -1):
        row_copy(place).start()
    for place in range(near, OWNERS):
        id_copy(place, place).wait_recv()
    look_up(near, OWNERS - near)
    for place in range(OWNERS - 1, near - 1, -1):
        row_copy(place).start()
    got[req] = rowbuf[0]

    asked_here = jnp.broadcast_to(ids[0, 0], (2 * PAIR, PAIR))
    giver = lax.div(lax.broadcasted_iota(I32, (2 * PAIR, PAIR), 0), 2 * CAP)
    order = jnp.transpose(ranked_hits(asked_here, giver)).astype(BF16)

    def wait_kv(head, carry):
        kv_copy(0, head).wait()
        kv_copy(1, head).wait()
        return carry

    lax.fori_loop(0, HEADS, wait_kv, 0)
    live = len_ref[0] - ctx * KEYS
    chunk = 256

    def cut(step, carry):
        start = pl.multiple_of(step * chunk, chunk)
        place = lax.broadcasted_iota(I32, (chunk, DH), 0) + start
        keep = jnp.where(place < live, 1.0, 0.0).astype(BF16)
        for head in range(HEADS):
            vals[head, pl.ds(start, chunk), :] = vals[head, pl.ds(start, chunk), :] * keep
        return carry

    lax.fori_loop(0, KEYS // chunk, cut, 0)
    for load in loads[1:]:
        load.wait()

    def came(peer):
        return pltpu.make_async_remote_copy(
            src_ref=rowbuf.at[0],
            dst_ref=got.at[peer],
            send_sem=row_send.at[0],
            recv_sem=row_recv.at[peer],
            device_id=(peer, ctx),
            device_id_type=MESH,
        )

    for place in others:
        came(peers[place]).wait_recv()
    emb[core] = jnp.dot(
        order, got[...].reshape(2 * PAIR, DE), preferred_element_type=F32
    ).astype(BF16)

    def emb_copy(source, block, there):
        return pltpu.make_async_remote_copy(
            src_ref=emb.at[source],
            dst_ref=emb.at[block],
            send_sem=emb_send.at[block],
            recv_sem=emb_recv.at[block],
            device_id=(req, there),
            device_id_type=MESH,
        )

    emb_given = emb_copy(core, core, partner)
    emb_given.start()
    def project(rows_in):
        features = jnp.dot(rows_in, w_in[...], preferred_element_type=F32).astype(BF16)
        normed = layer_norm(features.astype(F32)).astype(BF16)
        raw = jnp.dot(normed, w_uq[:, WIDTH:], preferred_element_type=F32)
        return features, normed, (silu(raw) * QSCALE).astype(BF16)

    def keep_query(buffer, scaled):
        for head in range(HEADS):
            buffer[head] = scaled[:, head * DH : (head + 1) * DH]

    my_rows = pl.ds(pl.multiple_of(core * HALF, HALF), HALF)
    their_rows = pl.ds(pl.multiple_of((1 - core) * HALF, HALF), HALF)

    def swap_copy(block, pair):
        heads = pl.ds(pair * 2, 2)
        return pltpu.make_async_remote_copy(
            src_ref=theirs.at[block, heads],
            dst_ref=swapped.at[block, heads],
            send_sem=swap_send.at[block, pair],
            recv_sem=swap_recv.at[block, pair],
            device_id=(req, partner),
            device_id_type=MESH,
        )

    def hand_over(block, pair, first):
        heads = pl.ds(pair * 2, 2)
        mine[block, heads] = acc[first : first + 2, my_rows, :]
        theirs[block, heads] = acc[first : first + 2, their_rows, :].astype(BF16)
        swap_copy(block, pair).start()

    def sum_copy(block, pair):
        heads = pl.ds(pair * 2, 2)
        return pltpu.make_async_remote_copy(
            src_ref=sums.at[block, heads],
            dst_ref=parts.at[block, heads],
            send_sem=part_send.at[block, pair],
            recv_sem=part_recv.at[block, pair],
            device_id=(req, (y, far, up, down)[block] * 2 + core),
            device_id_type=MESH,
        )

    def finish(block, pair):
        heads = pl.ds(pair * 2, 2)
        swap_copy(block, pair).wait_recv()
        sums[block, heads] = (mine[block, heads] + swapped[block, heads].astype(F32)).astype(BF16)
        sum_copy(block, pair).start()

    def weigh(score):
        return (score + score * jnp.tanh(score)).astype(BF16)

    piece = 512
    pieces = KEYS // piece

    def attend_two(quad):
        def scored(item):
            start = (item % pieces) * piece
            return lax.dot_general(
                keys[quad * 4 + item // pieces, start : start + piece, :],
                query_wide[quad * 4 + item // pieces],
                (((1,), (1,)), ((), ())),
                preferred_element_type=F32,
            )

        score = scored(0)
        total = None
        for item in range(4 * pieces):
            ahead = scored(item + 1) if item + 1 < 4 * pieces else None
            start = (item % pieces) * piece
            added = lax.dot_general(
                vals[quad * 4 + item // pieces, start : start + piece, :],
                weigh(score),
                (((0,), (0,)), ((), ())),
                preferred_element_type=F32,
            )
            total = added if item % pieces == 0 else total + added
            if item % pieces == pieces - 1:
                turned = jnp.transpose(total)
                acc[item // pieces] = turned[:PAIR]
                acc[4 + item // pieces] = turned[PAIR:]
            score = ahead
        for side in range(2):
            for part in range(2):
                hand_over(2 + side, quad * 2 + part, 4 * side + 2 * part)

    def attend_one(block, pair, count=1):
        for head in range(2 * count):
            score = lax.dot_general(
                query[block, pair * 2 + head],
                keys[pair * 2 + head],
                (((1,), (1,)), ((), ())),
                preferred_element_type=F32,
            )
            acc[head] = jnp.dot(
                weigh(score), vals[pair * 2 + head], preferred_element_type=F32
            )
        for part in range(count):
            hand_over(block, pair + part, 2 * part)

    def open_block(block):
        features, normed, scaled = project(emb[block])
        feat[block] = features
        norm[block] = normed
        keep_query(query.at[block], scaled)
        attend_one(block, 0)

    open_block(core)
    emb_copy(1 - core, 1 - core, partner).wait_recv()
    emb_copies = [emb_copy(0, 2, down * 2 + core), emb_copy(0, 3, up * 2 + core)]
    for copy in emb_copies:
        copy.start()
    open_block(1 - core)

    attend_one(1, 1, 3)
    finish(1, 0)

    for copy in emb_copies:
        copy.wait_recv()
    keep_query(query_wide, project(emb[2:4].reshape(2 * PAIR, DE))[2])

    def side_step(quad, carry):
        attend_two(quad)

        @pl.when(quad == 0)
        def _():
            for pair in range(1, 4):
                finish(1, pair)

        @pl.when(quad == 1)
        def _():
            for pair in range(2):
                finish(2, pair)
                finish(3, pair)

        return carry

    lax.fori_loop(0, 2, side_step, 0)

    def own_step(pair, carry):
        attend_one(0, pair)

        @pl.when(pair == 1)
        def _():
            for late in range(2, 4):
                finish(2, late)
                finish(3, late)

        return carry

    lax.fori_loop(1, 4, own_step, 0)

    gate = silu(
        jnp.dot(norm[0, my_rows, :], w_uq[:, :WIDTH], preferred_element_type=F32)
    ).astype(BF16)
    for pair in range(4):
        for block in range(1, 4):
            sum_copy(block, pair).wait_recv()
    mine[0] = mine[0] + sum(parts[block].astype(F32) for block in range(1, 4))
    for pair in range(3):
        swap_copy(0, pair).wait_recv()
    mine[0, :6] = mine[0, :6] + swapped[0, :6].astype(F32)
    swap_copy(0, 3).wait_recv()
    mine[0, 6:] = mine[0, 6:] + swapped[0, 6:].astype(F32)
    total = mine[0]
    attended = jnp.concatenate([total[head] for head in range(HEADS)], axis=-1)
    mixed = (layer_norm(attended) * gate.astype(F32)).astype(BF16)
    ranked = feat[0, my_rows, :].astype(F32) + jnp.dot(
        mixed, w_out[...], preferred_element_type=F32
    )
    out_ref[...] = ranked.astype(BF16)

    for place in others:
        id_copy(place, seen_from[place]).wait_send()
        row_copy(place).wait_send()
    for copy in [emb_given, *emb_copies]:
        copy.wait_send()
    for pair in range(4):
        for block in range(4):
            swap_copy(block, pair).wait_send()
        for block in range(1, 4):
            sum_copy(block, pair).wait_send()


def shards(item_table, cand_owner, cand_slot, w_in, w_uq, w_out, k_cache, v_cache, hist_len):
    hbm = pl.BlockSpec(memory_space=pl.ANY)
    vmem = pl.BlockSpec(memory_space=pltpu.VMEM)
    dma = pltpu.SemaphoreType.DMA
    out = pl.pallas_call(
        kernel,
        out_shape=pltpu.VMEM((HALF, WIDTH), BF16),
        in_specs=[hbm, hbm, pl.BlockSpec(memory_space=pltpu.SMEM)] + [hbm] * 6,
        out_specs=vmem,
        scratch_shapes=[
            pltpu.VMEM((OWNERS, 2, 1, PAIR), I32),
            pltpu.VMEM((ITEMS, DE), BF16),
            pltpu.VMEM((DE, WIDTH), BF16),
            pltpu.VMEM((WIDTH, 2 * WIDTH), BF16),
            pltpu.VMEM((WIDTH, WIDTH), BF16),
            pltpu.VMEM((HEADS, KEYS, DH), BF16),
            pltpu.VMEM((HEADS, KEYS, DH), BF16),
            pltpu.VMEM((OWNERS, 2 * CAP, DE), BF16),
            pltpu.VMEM((OWNERS, 2 * CAP, DE), BF16),
            pltpu.VMEM((4, PAIR, DE), BF16),
            pltpu.VMEM((2, PAIR, WIDTH), BF16),
            pltpu.VMEM((2, PAIR, WIDTH), BF16),
            pltpu.VMEM((2, HEADS, PAIR, DH), BF16),
            pltpu.VMEM((HEADS, 2 * PAIR, DH), BF16),
            pltpu.VMEM((8, PAIR, DH), F32),
            pltpu.VMEM((4, HEADS, HALF, DH), F32),
            pltpu.VMEM((4, HEADS, HALF, DH), BF16),
            pltpu.VMEM((4, HEADS, HALF, DH), BF16),
            pltpu.VMEM((4, HEADS, HALF, DH), BF16),
            pltpu.VMEM((4, HEADS, HALF, DH), BF16),
            dma((4,)),
            dma((2, HEADS)),
            dma((2,)),
            dma((OWNERS,)),
            dma((OWNERS,)),
            dma((OWNERS,)),
            dma((OWNERS,)),
            dma((4,)),
            dma((4,)),
            dma((4, 4)),
            dma((4, 4)),
            dma((4, 4)),
            dma((4, 4)),
        ],
        compiler_params=pltpu.CompilerParams(
            collective_id=0, has_side_effects=True, vmem_limit_bytes=56 * 2**20
        ),
    )(
        cand_owner.reshape(1, cand_owner.shape[1]),
        cand_slot,
        hist_len,
        item_table,
        w_in,
        w_uq,
        w_out,
        k_cache,
        v_cache,
    )
    return out[None]


def solution(mesh):
    in_specs = (
        P("req", None),
        P("req", None, None),
        P("req", None),
        P(),
        P(),
        P(),
        P("req", "ctx", None),
        P("req", "ctx", None),
        P("req"),
    )
    out_specs = P("req", "ctx", None)
    return jax.shard_map(shards, mesh=mesh, in_specs=in_specs, out_specs=out_specs, check_vma=False)
```
